32 devices in a mesh: groups: 2 (over x), spots: 16 (over z, y, core).
Axes of the slice: x: 2, y: 2, z: 4, core: 2. Of those that a mesh axis runs over, the one named last changes fastest.
Arguments:
- influence: float32 [8, 512, 128, 128], P(None, ('groups', 'spots')), parts along dimension 1, may hold values from 0 to 0.008
- spot_weights: float32 [16384], P(('groups', 'spots')), parts along dimension 0, may hold values from 0.2 to 2
- vox_block: int32 [8, 512], P(None, ('groups', 'spots')), parts along dimension 1, may hold values from 0 to 63, as said below
- spot_block: int32 [8, 512], P(None, ('groups', 'spots')), parts along dimension 1, may hold values from 0 to 3
- labels: int32 [16384], P(('groups', 'spots')), parts along dimension 0, may hold values from 0 to 7
- importance: float32 [16384], P(('groups', 'spots')), parts along dimension 0, may hold values from 1 to 400
- prescription: float32 [16], P('groups'), parts along dimension 0, may hold values from 0.3 to 1.5
Outputs:
- soft_worst: float32 [16384], P(('groups', 'spots')), parts along dimension 0
- gradient: float32 [16384], P(('groups', 'spots')), parts along dimension 0
The draws below stay inside these ranges and needn't reach their ends.
There are 2 independent parts, one for each index of `groups`. The reference program is written for one: setup_inputs(seed, part) draws one part's arguments, and reference() takes and returns one part's arrays. A program takes and returns all parts, laid end to end along the dimension named above; each array names one. Nothing has to cross between parts.
Inputs may be any that keep to these rules, and one draw needn't show every extreme that they name: `vox_block`: device p of the spots axis holds the stored blocks p * 16 to (p + 1) * 16 - 1; the first of them in each scenario names a voxel block of the owner (p + 16 / 2) mod 16, every other one a voxel block of an owner at most 4 indices from p (no block below 0 or past the end).
All inputs are finite; a program needn't handle non-finite values.
Results may differ from the reference program's by a relative error of at most 0.0003.
Values sent between devices are 32-bit elements; how exact they have to be, the bound alone decides.
A program may use at most 64 MiB of HBM per device.

```python
import math
import jax
import jax.numpy as jnp
from jax import lax

S = 8
BV = 128
BS = 128
NLAB = 8
REACH = 4
SB_DEV = 4
NNZ_DEV = 16
VB_DEV = 4
SPOTS = 8192
VB_TOT = 64
VOXELS = 8192
NB_TOT = 256
N_SPOTS = 16


def draw_vox_block(key, part):
    owners = NB_TOT // NNZ_DEV
    slot_ids = jnp.arange(NB_TOT, dtype=jnp.int32)
    device_ids = jnp.broadcast_to((slot_ids // NNZ_DEV)[None, :], (S, NB_TOT))
    slot_within = jnp.broadcast_to((slot_ids % NNZ_DEV)[None, :], (S, NB_TOT))
    key_off = jax.random.fold_in(key, 11)
    key_row = jax.random.fold_in(key, 12)
    offsets = jax.random.randint(key_off, (S, NB_TOT), -REACH, REACH + 1, dtype=jnp.int32)
    near_ids = jnp.clip(device_ids + offsets, 0, owners - 1)
    mirror_ids = (device_ids + owners // 2) % owners
    owner_ids = jnp.where(slot_within == 0, mirror_ids, near_ids)
    row_ids = jax.random.randint(key_row, (S, NB_TOT), 0, VB_DEV, dtype=jnp.int32)
    return (owner_ids * VB_DEV + row_ids).astype(jnp.int32)


def draw_importance(key, part):
    unit = jax.random.uniform(key, (VOXELS,), jnp.float32)
    values = jnp.exp(unit * jnp.log(8.0))
    return jnp.clip(values, 1.0, 400.0).astype(jnp.float32)


def with_ends(array, stream_key, smallest, largest):
    place = [jax.random.randint(jax.random.fold_in(stream_key, axis), (), 0, length) for axis, length in enumerate(array.shape)]
    widest = array.shape.index(max(array.shape))
    next_to = place[:widest] + [(place[widest] + 1) % array.shape[widest]] + place[widest + 1:]
    return array.at[tuple(place)].set(smallest).at[tuple(next_to)].set(largest)


def level_of(own_key, dims, cuts, least, largest):
    gain, own = 1.0, jax.random.fold_in(own_key, 6)
    for position, blocks in cuts:
        heights = jnp.exp(jax.random.uniform(jax.random.fold_in(own, position), (blocks,), jnp.float32, least / len(cuts), largest / len(cuts)))
        gain = gain * jnp.repeat(heights, dims[position] // blocks).reshape([-1 if axis == position else 1 for axis in range(len(dims))])
    return gain


def setup_inputs(seed: int = 0, part: int = 0) -> dict:
    key_list = jax.random.split(jax.random.key(seed), 8)
    own_keys = jax.random.split(jax.random.fold_in(key_list[7], part), 8)
    return {
        "influence": jnp.clip(0.008 * jax.random.uniform(own_keys[0], (S, NB_TOT, BV, BS), jnp.float32) ** level_of(own_keys[0], (S, NB_TOT, BV, BS), ((1, 16),), -0.2, 0.2), 0.0, 0.008),
        "spot_weights": jnp.clip(jnp.exp(math.log(2.0) - 2.3025851 * jax.random.uniform(own_keys[1], (SPOTS,), jnp.float32) ** level_of(own_keys[1], (SPOTS,), ((0, 16),), -0.2, 0.2)), 0.2, 2.0),
        "vox_block": draw_vox_block(jax.random.fold_in(jax.random.fold_in(key_list[7], part), 71), part),
        "spot_block": with_ends(jax.random.randint(own_keys[3], (S, NB_TOT), 0, SB_DEV), jax.random.fold_in(own_keys[3], 1), 0, SB_DEV - 1).astype(jnp.int32),
        "labels": with_ends(jax.random.randint(own_keys[4], (VOXELS,), 0, NLAB), jax.random.fold_in(own_keys[4], 1), 0, NLAB - 1).astype(jnp.int32),
        "importance": draw_importance(jax.random.fold_in(jax.random.fold_in(key_list[7], part), 71), part),
        "prescription": jnp.clip(jax.random.uniform(own_keys[6], (NLAB,), jnp.float32, 0.3, 1.5), 0.3, 1.5),
    }


def reference(influence, spot_weights, vox_block, spot_block, labels, importance, prescription):
    high = lax.Precision.HIGHEST
    slot_ids = jnp.arange(NB_TOT, dtype=jnp.int32)
    spot_global = (slot_ids // NNZ_DEV)[None, :] * SB_DEV + spot_block
    weight_rows = spot_weights.reshape(SB_DEV * N_SPOTS, BS)
    slot_input = weight_rows[spot_global]
    slot_dose = jnp.einsum("snvk,snk->snv", influence, slot_input, precision=high)
    scen_ids = jnp.broadcast_to(jnp.arange(S, dtype=jnp.int32)[:, None], (S, NB_TOT))
    dose_field = jnp.zeros((VB_TOT, S, BV), jnp.float32).at[vox_block, scen_ids].add(slot_dose)
    target = prescription[labels].reshape(VB_TOT, 1, BV)
    imp_rows = importance.reshape(VB_TOT, 1, BV)
    excess = dose_field - target
    score = imp_rows * excess * excess
    soft_worst = jax.nn.logsumexp(score, axis=1).reshape(VOXELS)
    dose_coef = jax.nn.softmax(score, axis=1) * 2.0 * imp_rows * excess
    slot_coef = dose_coef[vox_block, scen_ids]
    slot_grad = jnp.einsum("snvk,snv->snk", influence, slot_coef, precision=high)
    gradient = jnp.zeros((SB_DEV * N_SPOTS, BS), jnp.float32).at[spot_global].add(slot_grad)
    return soft_worst, gradient.reshape(SPOTS)
```

```python
import functools

import jax
import jax.numpy as jnp
from jax import lax
from jax.experimental import pallas as pl
from jax.experimental.pallas import tpu as pltpu
from jax.sharding import PartitionSpec as P

REACH = 4
NEAR = 2 * REACH + 1
F32 = jnp.float32
BF16 = jnp.bfloat16
MESH = pl.DeviceIdType.MESH


def split(x):
    hi = x.astype(BF16)
    lo = (x - hi.astype(F32)).astype(BF16)
    return hi, lo


def nt_dot(a, b):
    return lax.dot_general(a, b, (((1,), (1,)), ((), ())), preferred_element_type=F32)


def nn_dot(a, b):
    return lax.dot_general(a, b, (((1,), (0,)), ((), ())), preferred_element_type=F32)


def iota(shape, dim):
    return lax.broadcasted_iota(jnp.int32, shape, dim)


def kernel(
    inf_ref, w_ref, vox_ref, spot_ref, lab_ref, imp_ref, presc_ref,
    sw_ref, grad_ref,
    land, ihl, part, recv, coef, cbuf, pick,
    load_sem, send1, recv1, send2, recv2,
):
    scen, slots, rows, cols = land.shape
    vr = lab_ref.shape[0]
    sb = w_ref.shape[0]
    two = 8 // vr
    pairs = scen // two
    dests = NEAR + 1
    qrows = dests * 8
    n = lax.axis_size("spots")
    me = lax.axis_index("spots")
    mirror = lax.rem(me + n // 2, n)

    loads = [
        pltpu.make_async_copy(inf_ref.at[s], land.at[s], load_sem.at[s]) for s in range(scen)
    ]
    for load in loads:
        load.start()

    near = [e for e in range(-REACH, REACH + 1) if e != 0]

    def inside(e):
        return me + e >= 0 if e < 0 else me + e < n

    barrier = pltpu.get_barrier_semaphore()
    for e in near:
        @pl.when(inside(e))
        def _():
            pl.semaphore_signal(barrier, inc=1, device_id={"spots": me + e}, device_id_type=MESH)
    pl.semaphore_signal(barrier, inc=1, device_id={"spots": mirror}, device_id_type=MESH)

    for e in near:
        @pl.when(jnp.logical_not(inside(e)))
        def _():
            recv[e + REACH] = jnp.zeros(recv.shape[1:], F32)
            cbuf[e + REACH] = jnp.zeros(cbuf.shape[1:], F32)

    w_hi, w_lo = split(w_ref[...])
    w_rows = jnp.concatenate([w_hi.astype(F32), w_lo.astype(F32)], axis=0)
    parts = w_rows.shape[0]
    w_two = jnp.concatenate([w_rows, w_rows], axis=1).astype(BF16)

    vox = vox_ref[...]
    slot_id = iota(vox.shape, 1)
    rel = jnp.where(
        slot_id == 0,
        vox - vr * mirror + vr * NEAR,
        vox - vr * me + vr * REACH,
    )
    code = (rel * sb + spot_ref[...]).astype(F32).astype(BF16)
    width = slots * parts
    spread = (iota((slots, width), 1) // parts == iota((slots, width), 0)).astype(F32).astype(BF16)
    spread_t = (iota((width, slots), 0) // parts == iota((width, slots), 1)).astype(F32).astype(BF16)
    key = nn_dot(code, spread).astype(jnp.int32) - iota((scen, width), 1) % sb
    key_t = nt_dot(spread_t, code).astype(jnp.int32) - iota((width, scen), 0) % sb

    far = sb * vr * dests * 2

    def rel_of(q):
        return sb * ((q // 8) * vr + q % vr) + far * ((q % 8) // vr)

    q_id = iota((qrows, two * width), 0)
    row_code = rel_of(q_id)

    for sp in range(pairs):
        outs = []
        for s2 in range(two):
            s = sp * two + s2
            loads[s].wait()
            for b in range(slots):
                hi, lo = split(land[s, b])
                ihl[s, pl.ds(b * rows, rows), pl.ds(0, cols)] = hi
                ihl[s, pl.ds(b * rows, rows), pl.ds(cols, cols)] = lo
                outs.append(nt_dot(w_two, jnp.concatenate([hi, lo], axis=1)))
        dose = jnp.concatenate(outs, axis=0)
        key_row = jnp.concatenate(
            [key[sp * two + s2:sp * two + s2 + 1] + far * s2 for s2 in range(two)], axis=1
        )
        onto = (row_code == key_row).astype(F32).astype(BF16)
        d1 = dose.astype(BF16)
        rest = dose - d1.astype(F32)
        d2, d3 = split(rest)
        total = nn_dot(onto, d1) + (nn_dot(onto, d2) + nn_dot(onto, d3))
        part[:, sp] = total.reshape(dests, 8, rows)

    def copy_of(src, dst, send, rec, e):
        i = REACH + e
        return pltpu.make_async_remote_copy(
            src_ref=src(i), dst_ref=dst.at[REACH - e],
            send_sem=send.at[i], recv_sem=rec.at[REACH - e],
            device_id={"spots": me + e}, device_id_type=MESH,
        )

    def far_copy(src, dst, send, rec):
        return pltpu.make_async_remote_copy(
            src_ref=src(NEAR), dst_ref=dst.at[NEAR],
            send_sem=send.at[NEAR], recv_sem=rec.at[NEAR],
            device_id={"spots": mirror}, device_id_type=MESH,
        )

    def got(dst, send, rec, src, e):
        i = REACH + e
        return pltpu.make_async_remote_copy(
            src_ref=src(i), dst_ref=dst.at[i],
            send_sem=send.at[i], recv_sem=rec.at[i],
            device_id={"spots": me + e}, device_id_type=MESH,
        )

    expected = jnp.int32(1)
    for e in near:
        expected = expected + inside(e).astype(jnp.int32)
    pl.semaphore_wait(barrier, expected)

    order = sorted(near, key=lambda e: -abs(e))

    def exchange(src, dst, send, rec):
        far_copy(src, dst, send, rec).start()
        for e in order:
            @pl.when(inside(e))
            def _():
                copy_of(src, dst, send, rec, e).start()

    def arrive(src, dst, send, rec):
        for e in near:
            @pl.when(inside(e))
            def _():
                got(dst, send, rec, src, e).wait_recv()
        far_copy(src, dst, send, rec).wait_recv()

    def leave(src, dst, send, rec):
        for e in near:
            @pl.when(inside(e))
            def _():
                copy_of(src, dst, send, rec, e).wait_send()
        far_copy(src, dst, send, rec).wait_send()

    from_part = lambda i: part.at[i]
    from_coef = lambda i: coef
    exchange(from_part, recv, send1, recv1)

    lane = iota((width, 2 * 128), 1)
    line = iota((width, 2 * 128), 0)
    q = lane % 128
    lane_code = jnp.where(
        jnp.logical_and(lane // 128 == (line % parts) // sb, q < qrows), rel_of(q), -1000
    )
    for s in range(scen):
        pick[s] = (key_t[:, s:s + 1] + far * (s % two) == lane_code).astype(F32).astype(BF16)
    labels = lab_ref[...]
    target = jnp.zeros(labels.shape, F32)
    for k in range(presc_ref.shape[0]):
        target = jnp.where(labels == k, presc_ref[k], target)
    target = jnp.concatenate([target] * two, axis=0)
    imp = jnp.concatenate([imp_ref[...]] * two, axis=0)

    arrive(from_part, recv, send1, recv1)
    field = part[REACH]
    for i in range(dests):
        if i != REACH:
            field = field + recv[i]
    excess = field - target[None]
    score = imp[None] * excess * excess
    top = jnp.max(score, axis=0)
    top = jnp.maximum(top, pltpu.roll(top, vr, 0))
    expo = jnp.exp(score - top[None])
    whole = jnp.sum(expo, axis=0)
    whole = whole + pltpu.roll(whole, vr, 0)
    coef_now = expo / whole[None] * 2.0 * imp[None] * excess
    coef[...] = coef_now
    exchange(from_coef, cbuf, send2, recv2)
    sw_ref[...] = (top + jnp.log(whole))[:vr]
    cbuf[REACH] = coef_now

    arrive(from_coef, cbuf, send2, recv2)
    acc = jnp.zeros((parts, 2 * cols), F32)
    pad = jnp.zeros((128 - qrows, rows), BF16)
    for sp in range(pairs):
        c_hi, c_lo = split(cbuf[:, sp].reshape(qrows, rows))
        c_two = jnp.concatenate([c_hi, pad, c_lo, pad], axis=0)
        for s2 in range(two):
            s = sp * two + s2
            tiles = nn_dot(pick[s], c_two)
            left = jnp.concatenate(
                [tiles[b * parts:(b + 1) * parts] for b in range(slots)], axis=1
            ).astype(BF16)
            acc = acc + nn_dot(left, ihl[s])
    acc = acc[:, :cols] + acc[:, cols:]
    grad_ref[...] = acc[:sb] + acc[sb:]

    leave(from_part, recv, send1, recv1)
    leave(from_coef, cbuf, send2, recv2)


def per_device(influence, spot_weights, vox_block, spot_block, labels, importance, prescription):
    scen, slots, rows, cols = influence.shape
    sb = spot_weights.shape[0] // cols
    vr = labels.shape[0] // rows
    assert 8 % vr == 0 and 2 * vr == 8 and scen % 2 == 0 and 2 * sb == 8
    slab = (scen * vr // 8, 8, rows)
    dests = NEAR + 1
    vmem = pl.BlockSpec(memory_space=pltpu.VMEM)
    worst, gradient = pl.pallas_call(
        kernel,
        out_shape=(
            jax.ShapeDtypeStruct((vr, rows), F32),
            jax.ShapeDtypeStruct((sb, cols), F32),
        ),
        in_specs=[pl.BlockSpec(memory_space=pl.ANY)] + [vmem] * 5
        + [pl.BlockSpec(memory_space=pltpu.SMEM)],
        out_specs=(vmem, vmem),
        scratch_shapes=[
            pltpu.VMEM((scen, slots, rows, cols), F32),
            pltpu.VMEM((scen, slots * rows, 2 * cols), BF16),
            pltpu.VMEM((dests,) + slab, F32),
            pltpu.VMEM((dests,) + slab, F32),
            pltpu.VMEM(slab, F32),
            pltpu.VMEM((dests,) + slab, F32),
            pltpu.VMEM((scen, slots * 2 * sb, 256), BF16),
            pltpu.SemaphoreType.DMA((scen,)),
            pltpu.SemaphoreType.DMA((dests,)),
            pltpu.SemaphoreType.DMA((dests,)),
            pltpu.SemaphoreType.DMA((dests,)),
            pltpu.SemaphoreType.DMA((dests,)),
        ],
        compiler_params=pltpu.CompilerParams(
            collective_id=0, has_side_effects=True, vmem_limit_bytes=56 * 1024 * 1024
        ),
    )(
        influence, spot_weights.reshape(sb, cols), vox_block, spot_block,
        labels.reshape(vr, rows), importance.reshape(vr, rows), prescription,
    )
    return worst.reshape(vr * rows), gradient.reshape(sb * cols)


def solution(mesh):
    both = P(("groups", "spots"))
    in_specs = (
        P(None, ("groups", "spots"), None, None),
        both,
        P(None, ("groups", "spots")),
        P(None, ("groups", "spots")),
        both,
        both,
        P("groups"),
    )
    return jax.shard_map(
        per_device, mesh=mesh, in_specs=in_specs, out_specs=(both, both), check_vma=False
    )
```

```python
import functools

import jax
import jax.numpy as jnp
from jax import lax
from jax.experimental import pallas as pl
from jax.experimental.pallas import tpu as pltpu
from jax.sharding import PartitionSpec as P

REACH = 4
NEAR = 2 * REACH + 1
F32 = jnp.float32
BF16 = jnp.bfloat16
MESH = pl.DeviceIdType.MESH


def split(x):
    hi = x.astype(BF16)
    lo = (x - hi.astype(F32)).astype(BF16)
    return hi, lo


def nt_dot(a, b):
    return lax.dot_general(a, b, (((1,), (1,)), ((), ())), preferred_element_type=F32)


def nn_dot(a, b):
    return lax.dot_general(a, b, (((1,), (0,)), ((), ())), preferred_element_type=F32)


def iota(shape, dim):
    return lax.broadcasted_iota(jnp.int32, shape, dim)


def kernel(
    inf_ref, w_in, vox_in, spot_in, lab_in, imp_in, presc_in,
    out_ref,
    w_ref, vox_ref, spot_ref, lab_ref, imp_ref, presc_ref, small_sem,
    land, ihl, part, recv, coef, cbuf, pick,
    load_sem, send1, recv1, send2, recv2,
):
    scen, slots, rows, cols = land.shape
    vr = lab_ref.shape[0]
    sb = w_ref.shape[0]
    two = 8 // vr
    pairs = scen // two
    dests = NEAR + 1
    qrows = dests * 8
    n = lax.axis_size("spots")
    me = lax.axis_index("spots")
    mirror = lax.rem(me + n // 2, n)

    loads = [
        pltpu.make_async_copy(inf_ref.at[s], land.at[s], load_sem.at[s]) for s in range(scen)
    ]
    small = [
        pltpu.make_async_copy(src, dst, small_sem.at[i])
        for i, (src, dst) in enumerate((
            (w_in, w_ref), (vox_in, vox_ref), (spot_in, spot_ref),
            (lab_in, lab_ref), (imp_in, imp_ref), (presc_in, presc_ref),
        ))
    ]
    for load in small[:3] + loads + small[3:]:
        load.start()

    near = [e for e in range(-REACH, REACH + 1) if e != 0]

    def inside(e):
        return me + e >= 0 if e < 0 else me + e < n

    barrier = pltpu.get_barrier_semaphore()
    for e in near:
        @pl.when(inside(e))
        def _():
            pl.semaphore_signal(barrier, inc=1, device_id={"spots": me + e}, device_id_type=MESH)
    pl.semaphore_signal(barrier, inc=1, device_id={"spots": mirror}, device_id_type=MESH)

    for e in near:
        @pl.when(jnp.logical_not(inside(e)))
        def _():
            recv[e + REACH] = jnp.zeros(recv.shape[1:], F32)
            cbuf[e + REACH] = jnp.zeros(cbuf.shape[1:], F32)

    for load in small[:3]:
        load.wait()

    w_hi, w_lo = split(w_ref[...])
    w_rows = jnp.concatenate([w_hi.astype(F32), w_lo.astype(F32)], axis=0)
    parts = w_rows.shape[0]
    w_two = jnp.concatenate([w_rows, w_rows], axis=1).astype(BF16)

    vox = vox_ref[...]
    slot_id = iota(vox.shape, 1)
    rel = jnp.where(
        slot_id == 0,
        vox - vr * mirror + vr * NEAR,
        vox - vr * me + vr * REACH,
    )
    code = (rel * sb + spot_ref[...]).astype(F32).astype(BF16)
    width = slots * parts
    spread = (iota((slots, width), 1) // parts == iota((slots, width), 0)).astype(F32).astype(BF16)
    spread_t = (iota((width, slots), 0) // parts == iota((width, slots), 1)).astype(F32).astype(BF16)
    key = nn_dot(code, spread).astype(jnp.int32) - iota((scen, width), 1) % sb
    key_t = nt_dot(spread_t, code).astype(jnp.int32) - iota((width, scen), 0) % sb

    far = sb * vr * dests * 2

    def rel_of(q):
        return sb * ((q // 8) * vr + q % vr) + far * ((q % 8) // vr)

    q_id = iota((qrows, two * width), 0)
    row_code = rel_of(q_id)

    for sp in range(pairs):
        outs = []
        for s2 in range(two):
            s = sp * two + s2
            loads[s].wait()
            for b in range(slots):
                hi, lo = split(land[s, b])
                ihl[s, pl.ds(b * rows, rows), pl.ds(0, cols)] = hi
                ihl[s, pl.ds(b * rows, rows), pl.ds(cols, cols)] = lo
            for b in range(slots):
                outs.append(nt_dot(w_two, ihl[s, pl.ds(b * rows, rows)]))
        dose = jnp.concatenate(outs, axis=0)
        key_row = jnp.concatenate(
            [key[sp * two + s2:sp * two + s2 + 1] + far * s2 for s2 in range(two)], axis=1
        )
        onto = (row_code == key_row).astype(F32).astype(BF16)
        d1 = dose.astype(BF16)
        rest = dose - d1.astype(F32)
        d2, d3 = split(rest)
        total = nn_dot(onto, d1) + (nn_dot(onto, d2) + nn_dot(onto, d3))
        part[:, sp] = total.reshape(dests, 8, rows)

    def copy_of(src, dst, send, rec, e):
        i = REACH + e
        return pltpu.make_async_remote_copy(
            src_ref=src(i), dst_ref=dst.at[REACH - e],
            send_sem=send.at[i], recv_sem=rec.at[REACH - e],
            device_id={"spots": me + e}, device_id_type=MESH,
        )

    def far_copy(src, dst, send, rec):
        return pltpu.make_async_remote_copy(
            src_ref=src(NEAR), dst_ref=dst.at[NEAR],
            send_sem=send.at[NEAR], recv_sem=rec.at[NEAR],
            device_id={"spots": mirror}, device_id_type=MESH,
        )

    def got(dst, send, rec, src, e):
        i = REACH + e
        return pltpu.make_async_remote_copy(
            src_ref=src(i), dst_ref=dst.at[i],
            send_sem=send.at[i], recv_sem=rec.at[i],
            device_id={"spots": me + e}, device_id_type=MESH,
        )

    expected = jnp.int32(1)
    for e in near:
        expected = expected + inside(e).astype(jnp.int32)
    pl.semaphore_wait(barrier, expected)

    order = sorted(near, key=lambda e: -abs(e))

    def exchange(src, dst, send, rec):
        far_copy(src, dst, send, rec).start()
        for e in order:
            @pl.when(inside(e))
            def _():
                copy_of(src, dst, send, rec, e).start()

    def arrive(src, dst, send, rec):
        for e in near:
            @pl.when(inside(e))
            def _():
                got(dst, send, rec, src, e).wait_recv()
        far_copy(src, dst, send, rec).wait_recv()

    def leave(src, dst, send, rec):
        for e in near:
            @pl.when(inside(e))
            def _():
                copy_of(src, dst, send, rec, e).wait_send()
        far_copy(src, dst, send, rec).wait_send()

    from_part = lambda i: part.at[i]
    from_coef = lambda i: coef
    exchange(from_part, recv, send1, recv1)

    lane = iota((width, 2 * 128), 1)
    line = iota((width, 2 * 128), 0)
    q = lane % 128
    lane_code = jnp.where(
        jnp.logical_and(lane // 128 == (line % parts) // sb, q < qrows), rel_of(q), -1000
    )
    for s in range(scen):
        pick[s] = (key_t[:, s:s + 1] + far * (s % two) == lane_code).astype(F32).astype(BF16)
    for load in small[3:]:
        load.wait()
    labels = lab_ref[...]
    target = jnp.zeros(labels.shape, F32)
    for k in range(presc_ref.shape[0]):
        target = jnp.where(labels == k, presc_ref[k], target)
    target = jnp.concatenate([target] * two, axis=0)
    imp = jnp.concatenate([imp_ref[...]] * two, axis=0)

    arrive(from_part, recv, send1, recv1)
    field = part[REACH]
    for i in range(dests):
        if i != REACH:
            field = field + recv[i]
    excess = field - target[None]
    score = imp[None] * excess * excess
    top = jnp.max(score, axis=0)
    top = jnp.maximum(top, pltpu.roll(top, vr, 0))
    expo = jnp.exp(score - top[None])
    whole = jnp.sum(expo, axis=0)
    whole = whole + pltpu.roll(whole, vr, 0)
    coef_now = expo / whole[None] * 2.0 * imp[None] * excess
    coef[...] = coef_now
    exchange(from_coef, cbuf, send2, recv2)
    out_ref[pl.ds(0, vr)] = (top + jnp.log(whole))[:vr]
    cbuf[REACH] = coef_now

    arrive(from_coef, cbuf, send2, recv2)
    sums = []
    pad = jnp.zeros((128 - qrows, rows), BF16)
    for sp in range(pairs):
        c_hi, c_lo = split(cbuf[:, sp].reshape(qrows, rows))
        c_two = jnp.concatenate([c_hi, pad, c_lo, pad], axis=0)
        for s2 in range(two):
            s = sp * two + s2
            tiles = nn_dot(pick[s], c_two)
            left = jnp.concatenate(
                [tiles[b * parts:(b + 1) * parts] for b in range(slots)], axis=1
            ).astype(BF16)
            sums.append(nn_dot(left, ihl[s]))
    while len(sums) > 1:
        sums = [sums[i] + sums[i + 1] for i in range(0, len(sums), 2)]
    acc = sums[0]
    acc = acc[:, :cols] + acc[:, cols:]
    out_ref[pl.ds(vr, sb)] = acc[:sb] + acc[sb:]

    leave(from_part, recv, send1, recv1)
    leave(from_coef, cbuf, send2, recv2)


def per_device(influence, spot_weights, vox_block, spot_block, labels, importance, prescription):
    scen, slots, rows, cols = influence.shape
    sb = spot_weights.shape[0] // cols
    vr = labels.shape[0] // rows
    assert 8 % vr == 0 and 2 * vr == 8 and scen % 2 == 0 and 2 * sb == 8
    slab = (scen * vr // 8, 8, rows)
    dests = NEAR + 1
    vmem = pl.BlockSpec(memory_space=pltpu.VMEM)
    both = pl.pallas_call(
        kernel,
        out_shape=jax.ShapeDtypeStruct((vr + sb, rows), F32),
        in_specs=[pl.BlockSpec(memory_space=pl.ANY)] * 7,
        out_specs=vmem,
        scratch_shapes=[
            pltpu.VMEM((sb, cols), F32),
            pltpu.VMEM(vox_block.shape, jnp.int32),
            pltpu.VMEM(spot_block.shape, jnp.int32),
            pltpu.VMEM((vr, rows), jnp.int32),
            pltpu.VMEM((vr, rows), F32),
            pltpu.SMEM(prescription.shape, F32),
            pltpu.SemaphoreType.DMA((6,)),
            pltpu.VMEM((scen, slots, rows, cols), F32),
            pltpu.VMEM((scen, slots * rows, 2 * cols), BF16),
            pltpu.VMEM((dests,) + slab, F32),
            pltpu.VMEM((dests,) + slab, F32),
            pltpu.VMEM(slab, F32),
            pltpu.VMEM((dests,) + slab, F32),
            pltpu.VMEM((scen, slots * 2 * sb, 256), BF16),
            pltpu.SemaphoreType.DMA((scen,)),
            pltpu.SemaphoreType.DMA((dests,)),
            pltpu.SemaphoreType.DMA((dests,)),
            pltpu.SemaphoreType.DMA((dests,)),
            pltpu.SemaphoreType.DMA((dests,)),
        ],
        compiler_params=pltpu.CompilerParams(
            collective_id=0, has_side_effects=True, vmem_limit_bytes=56 * 1024 * 1024
        ),
    )(
        influence, spot_weights.reshape(sb, cols), vox_block, spot_block,
        labels.reshape(vr, rows), importance.reshape(vr, rows), prescription,
    )
    return both[:vr].reshape(vr * rows), both[vr:].reshape(sb * cols)


def solution(mesh):
    both = P(("groups", "spots"))
    in_specs = (
        P(None, ("groups", "spots"), None, None),
        both,
        P(None, ("groups", "spots")),
        P(None, ("groups", "spots")),
        both,
        both,
        P("groups"),
    )
    return jax.shard_map(
        per_device, mesh=mesh, in_specs=in_specs, out_specs=(both, both), check_vma=False
    )
```

```python
import functools

import jax
import jax.numpy as jnp
from jax import lax
from jax.experimental import pallas as pl
from jax.experimental.pallas import tpu as pltpu
from jax.sharding import PartitionSpec as P

REACH = 4
NEAR = 2 * REACH + 1
F32 = jnp.float32
BF16 = jnp.bfloat16
MESH = pl.DeviceIdType.MESH


def split(x):
    hi = x.astype(BF16)
    lo = (x - hi.astype(F32)).astype(BF16)
    return hi, lo


def nt_dot(a, b):
    return lax.dot_general(a, b, (((1,), (1,)), ((), ())), preferred_element_type=F32)


def nn_dot(a, b):
    return lax.dot_general(a, b, (((1,), (0,)), ((), ())), preferred_element_type=F32)


def iota(shape, dim):
    return lax.broadcasted_iota(jnp.int32, shape, dim)


def kernel(
    inf_ref, w_in, vox_in, spot_in, lab_in, imp_in, presc_in,
    out_ref,
    w_ref, vox_ref, spot_ref, lab_ref, imp_ref, presc_ref, small_sem,
    land, ihl, part, recv, coef, cbuf, pick,
    load_sem, send1, recv1, send2, recv2,
):
    scen, slots, rows, cols = land.shape
    vr = lab_ref.shape[0]
    sb = w_ref.shape[0]
    two = 8 // vr
    pairs = scen // two
    dests = NEAR + 1
    qrows = dests * 8
    n = lax.axis_size("spots")
    me = lax.axis_index("spots")
    mirror = lax.rem(me + n // 2, n)

    loads = [
        pltpu.make_async_copy(inf_ref.at[s], land.at[s], load_sem.at[s]) for s in range(scen)
    ]
    small = [
        pltpu.make_async_copy(src, dst, small_sem.at[i])
        for i, (src, dst) in enumerate((
            (w_in, w_ref), (vox_in, vox_ref), (spot_in, spot_ref),
            (lab_in, lab_ref), (imp_in, imp_ref), (presc_in, presc_ref),
        ))
    ]
    for load in small[:3] + loads + small[3:]:
        load.start()

    near = [e for e in range(-REACH, REACH + 1) if e != 0]

    def inside(e):
        return me + e >= 0 if e < 0 else me + e < n

    barrier = pltpu.get_barrier_semaphore()
    for e in near:
        @pl.when(inside(e))
        def _():
            pl.semaphore_signal(barrier, inc=1, device_id={"spots": me + e}, device_id_type=MESH)
    pl.semaphore_signal(barrier, inc=1, device_id={"spots": mirror}, device_id_type=MESH)

    for e in near:
        @pl.when(jnp.logical_not(inside(e)))
        def _():
            recv[e + REACH] = jnp.zeros(recv.shape[1:], F32)
            cbuf[e + REACH] = jnp.zeros(cbuf.shape[1:], F32)

    for load in small[:3]:
        load.wait()

    w_hi, w_lo = split(w_ref[...])
    w_rows = jnp.concatenate([w_hi.astype(F32), w_lo.astype(F32)], axis=0)
    parts = w_rows.shape[0]
    w_two = jnp.concatenate([w_rows, w_rows], axis=1).astype(BF16)

    vox = vox_ref[...]
    slot_id = iota(vox.shape, 1)
    rel = jnp.where(
        slot_id == 0,
        vox - vr * mirror + vr * NEAR,
        vox - vr * me + vr * REACH,
    )
    code = (rel * sb + spot_ref[...]).astype(F32).astype(BF16)
    width = slots * parts
    spread = (iota((slots, width), 1) // parts == iota((slots, width), 0)).astype(F32).astype(BF16)
    spread_t = (iota((width, slots), 0) // parts == iota((width, slots), 1)).astype(F32).astype(BF16)
    key = nn_dot(code, spread).astype(jnp.int32) - iota((scen, width), 1) % sb
    key_t = nt_dot(spread_t, code).astype(jnp.int32) - iota((width, scen), 0) % sb

    far = sb * vr * dests * 2

    def rel_of(q):
        return sb * ((q // 8) * vr + q % vr) + far * ((q % 8) // vr)

    q_id = iota((qrows, two * width), 0)
    row_code = rel_of(q_id)

    for sp in range(pairs):
        outs = []
        for s2 in range(two):
            s = sp * two + s2
            loads[s].wait()
            for b in range(slots):
                hi, lo = split(land[s, b])
                ihl[s, pl.ds(b * rows, rows), pl.ds(0, cols)] = hi
                ihl[s, pl.ds(b * rows, rows), pl.ds(cols, cols)] = lo
            for b in range(slots):
                outs.append(nt_dot(w_two, ihl[s, pl.ds(b * rows, rows)]))
        dose = jnp.concatenate(outs, axis=0)
        key_row = jnp.concatenate(
            [key[sp * two + s2:sp * two + s2 + 1] + far * s2 for s2 in range(two)], axis=1
        )
        onto = (row_code == key_row).astype(F32).astype(BF16)
        d1 = dose.astype(BF16)
        rest = dose - d1.astype(F32)
        d2, d3 = split(rest)
        total = nn_dot(onto, d1) + (nn_dot(onto, d2) + nn_dot(onto, d3))
        part[:, sp] = total.reshape(dests, 8, rows)

    def copy_of(src, dst, send, rec, e):
        i = REACH + e
        return pltpu.make_async_remote_copy(
            src_ref=src(i), dst_ref=dst.at[REACH - e],
            send_sem=send.at[i], recv_sem=rec.at[REACH - e],
            device_id={"spots": me + e}, device_id_type=MESH,
        )

    def far_copy(src, dst, send, rec):
        return pltpu.make_async_remote_copy(
            src_ref=src(NEAR), dst_ref=dst.at[NEAR],
            send_sem=send.at[NEAR], recv_sem=rec.at[NEAR],
            device_id={"spots": mirror}, device_id_type=MESH,
        )

    def got(dst, send, rec, src, e):
        i = REACH + e
        return pltpu.make_async_remote_copy(
            src_ref=src(i), dst_ref=dst.at[i],
            send_sem=send.at[i], recv_sem=rec.at[i],
            device_id={"spots": me + e}, device_id_type=MESH,
        )

    expected = jnp.int32(1)
    for e in near:
        expected = expected + inside(e).astype(jnp.int32)
    pl.semaphore_wait(barrier, expected)

    order = sorted(near, key=lambda e: -abs(e))

    def exchange(src, dst, send, rec):
        far_copy(src, dst, send, rec).start()
        for e in order:
            @pl.when(inside(e))
            def _():
                copy_of(src, dst, send, rec, e).start()

    def arrive(src, dst, send, rec):
        for e in near:
            @pl.when(inside(e))
            def _():
                got(dst, send, rec, src, e).wait_recv()
        far_copy(src, dst, send, rec).wait_recv()

    def leave(src, dst, send, rec):
        for e in near:
            @pl.when(inside(e))
            def _():
                copy_of(src, dst, send, rec, e).wait_send()
        far_copy(src, dst, send, rec).wait_send()

    from_part = lambda i: part.at[i]
    from_coef = lambda i: coef
    exchange(from_part, recv, send1, recv1)

    lane = iota((width, 2 * 128), 1)
    line = iota((width, 2 * 128), 0)
    q = lane % 128
    lane_code = jnp.where(
        jnp.logical_and(lane // 128 == (line % parts) // sb, q < qrows), rel_of(q), -1000
    )
    for s in range(scen):
        pick[s] = (key_t[:, s:s + 1] + far * (s % two) == lane_code).astype(F32).astype(BF16)
    for load in small[3:]:
        load.wait()
    labels = lab_ref[...]
    target = jnp.zeros(labels.shape, F32)
    for k in range(presc_ref.shape[0]):
        target = jnp.where(labels == k, presc_ref[k], target)
    target = jnp.concatenate([target] * two, axis=0)
    imp = jnp.concatenate([imp_ref[...]] * two, axis=0)

    arrive(from_part, recv, send1, recv1)
    field = part[REACH]
    for i in range(dests):
        if i != REACH:
            field = field + recv[i]
    excess = field - target[None]
    score = imp[None] * excess * excess
    top = jnp.max(score, axis=0)
    top = jnp.maximum(top, pltpu.roll(top, vr, 0))
    expo = jnp.exp(score - top[None])
    whole = jnp.sum(expo, axis=0)
    whole = whole + pltpu.roll(whole, vr, 0)
    coef_now = expo / whole[None] * 2.0 * imp[None] * excess
    coef[...] = coef_now
    exchange(from_coef, cbuf, send2, recv2)
    out_ref[pl.ds(0, vr)] = (top + jnp.log(whole))[:vr]
    cbuf[REACH] = coef_now

    arrive(from_coef, cbuf, send2, recv2)
    def back(sp, acc):
        c_hi, c_lo = split(cbuf[:, sp].reshape(qrows, rows))
        c_two = jnp.concatenate([c_hi, pad, c_lo, pad], axis=0)
        sums = []
        for s2 in range(two):
            tiles = nn_dot(pick[sp * two + s2], c_two)
            left = jnp.concatenate(
                [tiles[b * parts:(b + 1) * parts] for b in range(slots)], axis=1
            ).astype(BF16)
            sums.append(nn_dot(left, ihl[sp * two + s2]))
        return acc + (sums[0] + sums[1])

    pad = jnp.zeros((128 - qrows, rows), BF16)
    acc = lax.fori_loop(0, pairs, back, jnp.zeros((parts, 2 * cols), F32))
    acc = acc[:, :cols] + acc[:, cols:]
    out_ref[pl.ds(vr, sb)] = acc[:sb] + acc[sb:]

    leave(from_part, recv, send1, recv1)
    leave(from_coef, cbuf, send2, recv2)


def per_device(influence, spot_weights, vox_block, spot_block, labels, importance, prescription):
    scen, slots, rows, cols = influence.shape
    sb = spot_weights.shape[0] // cols
    vr = labels.shape[0] // rows
    assert 8 % vr == 0 and 2 * vr == 8 and scen % 2 == 0 and 2 * sb == 8
    slab = (scen * vr // 8, 8, rows)
    dests = NEAR + 1
    vmem = pl.BlockSpec(memory_space=pltpu.VMEM)
    both = pl.pallas_call(
        kernel,
        out_shape=jax.ShapeDtypeStruct((vr + sb, rows), F32),
        in_specs=[pl.BlockSpec(memory_space=pl.ANY)] * 7,
        out_specs=vmem,
        scratch_shapes=[
            pltpu.VMEM((sb, cols), F32),
            pltpu.VMEM(vox_block.shape, jnp.int32),
            pltpu.VMEM(spot_block.shape, jnp.int32),
            pltpu.VMEM((vr, rows), jnp.int32),
            pltpu.VMEM((vr, rows), F32),
            pltpu.SMEM(prescription.shape, F32),
            pltpu.SemaphoreType.DMA((6,)),
            pltpu.VMEM((scen, slots, rows, cols), F32),
            pltpu.VMEM((scen, slots * rows, 2 * cols), BF16),
            pltpu.VMEM((dests,) + slab, F32),
            pltpu.VMEM((dests,) + slab, F32),
            pltpu.VMEM(slab, F32),
            pltpu.VMEM((dests,) + slab, F32),
            pltpu.VMEM((scen, slots * 2 * sb, 256), BF16),
            pltpu.SemaphoreType.DMA((scen,)),
            pltpu.SemaphoreType.DMA((dests,)),
            pltpu.SemaphoreType.DMA((dests,)),
            pltpu.SemaphoreType.DMA((dests,)),
            pltpu.SemaphoreType.DMA((dests,)),
        ],
        compiler_params=pltpu.CompilerParams(
            collective_id=0, has_side_effects=True, vmem_limit_bytes=56 * 1024 * 1024
        ),
    )(
        influence, spot_weights.reshape(sb, cols), vox_block, spot_block,
        labels.reshape(vr, rows), importance.reshape(vr, rows), prescription,
    )
    return both[:vr].reshape(vr * rows), both[vr:].reshape(sb * cols)


def solution(mesh):
    both = P(("groups", "spots"))
    in_specs = (
        P(None, ("groups", "spots"), None, None),
        both,
        P(None, ("groups", "spots")),
        P(None, ("groups", "spots")),
        both,
        both,
        P("groups"),
    )
    return jax.shard_map(
        per_device, mesh=mesh, in_specs=in_specs, out_specs=(both, both), check_vma=False
    )
```
